32 devices in a mesh: replica: 2 (over y), shard: 16 (over z, x, core).
Axes of the slice: x: 2, y: 2, z: 4, core: 2. Of those that a mesh axis runs over, the one named last changes fastest.
Arguments:
- tokens: bfloat16 [16384, 2048], P(('replica', 'shard')), may hold values from -6 to 6
- block_ids: int32 [32, 512], P(('replica', 'shard')), may hold values from 0 to 3, never falling along the last dimension, each value on 1 to 256 neighbouring positions
- query_weight: bfloat16 [2048, 2048], P('shard'), may hold values from -0.47851562 to 0.47851562
- key_projection_weight: bfloat16 [2048, 512], P('shard'), may hold values from -0.47851562 to 0.47851562
- value_projection_weight: bfloat16 [2048, 512], P('shard'), may hold values from -0.125 to 0.125
- output_weight: bfloat16 [2048, 2048], P('shard'), may hold values from -2.390625 to 2.390625
- gate_weight: bfloat16 [2048, 8192], P('shard'), may hold values from -0.125 to 0.125
- up_weight: bfloat16 [2048, 8192], P('shard'), may hold values from -0.125 to 0.125
- down_weight: bfloat16 [8192, 2048], P('shard'), may hold values from -0.359375 to 0.359375
- attn_gain: bfloat16 [2048], P('shard'), may hold values from 0.5 to 1.5
- mlp_gain: bfloat16 [2048], P('shard'), may hold values from 0.5 to 1.5
- cotangent: bfloat16 [16384, 2048], P(('replica', 'shard')), may hold values from -6 to 6
Outputs:
- output: bfloat16 [16384, 2048], P(('replica', 'shard'))
- input_grad: float32 [16384, 2048], P(('replica', 'shard'))
- query_grad: float32 [2048, 2048], P('shard')
- key_grad: float32 [2048, 512], P('shard')
- value_grad: float32 [2048, 512], P('shard')
- output_grad: float32 [2048, 2048], P('shard')
- gate_grad: float32 [2048, 8192], P('shard')
- up_grad: float32 [2048, 8192], P('shard')
- down_grad: float32 [8192, 2048], P('shard')
- attn_gain_grad: float32 [2048], P('shard')
- mlp_gain_grad: float32 [2048], P('shard')
The draws below stay inside these ranges and needn't reach their ends.
Inputs may be any that keep to these rules, and one draw needn't show every extreme that they name: `block_ids`: in each row the ids start at 0 and never fall, every id of 0 to 3 appears, a block holds 1 to 256 tokens and one block of every row holds exactly 256.
All inputs are finite; a program needn't handle non-finite values.
Results may differ from the reference program's by a relative error of at most 0.015.
Values may be sent and summed in bfloat16 or wider, within the bound.
No kernel may reach another device: no remote copies, remote signals or barrier semaphores. Data moves between devices by JAX's collectives and lax.ppermute only.
A program may use at most 576 MiB of HBM per device.

```python
import math
import jax
import jax.numpy as jnp
import numpy as np
from jax import lax

MODEL_WIDTH = 2048
QUERY_HEADS = 32
KEY_VALUE_HEADS = 8
HEAD_WIDTH = 64
FF = 8192
SEQ_LEN = 512
BLOCK = 256
BLOCKS = 4
SEQS = 32
TOKENS = 16384


def block_scale(rng, dims, shards, low, high):
    def one(dim, parts):
        steps = jax.random.uniform(jax.random.fold_in(jax.random.fold_in(rng, 6), dim), (parts,), jnp.float32, low / len(shards), high / len(shards))
        return jnp.repeat(jnp.exp(steps), dims[dim] // parts).reshape((-1,) + (1,) * (len(dims) - dim - 1))

    loudness = one(*shards[0])
    for cut in shards[1:]:
        loudness = loudness * one(*cut)
    return loudness


def split_up(count, total, most, skew):
    weights = [(1 << 20) // math.isqrt(grade ** skew) + 1 for grade in range(2, count + 1)]
    surplus, counts = total - most - (count - 1), [1] * (count - 1)
    while surplus > 0:
        movable = [i for i in range(count - 1) if counts[i] < most]
        mass, left = sum([weights[i] for i in movable]), surplus
        for i in movable:
            addition = min(most - counts[i], max(1, left * weights[i] // mass), surplus)
            counts[i] = counts[i] + addition
            surplus = surplus - addition
    return np.array([most] + counts)


def ragged(own_key, number_of, total, most, skew):
    if number_of == 2:
        one = jax.random.randint(own_key, (), max(1, total - most), min(most, total - 1) + 1)
        return jnp.stack([one, total - one])
    sizes = jnp.asarray(split_up(number_of, total, most, skew), jnp.int32)
    twos = (number_of - 1) // 2
    giver, sink = sizes[1:1 + 2 * twos:2], sizes[2:2 + 2 * twos:2]
    margin = jnp.minimum(giver - 1, most - sink)
    passed = jax.random.randint(jax.random.fold_in(own_key, 1), (twos,), 0, 1 << 20) % (margin + 1)
    sizes = sizes.at[1:1 + 2 * twos:2].set(giver - passed).at[2:2 + 2 * twos:2].set(sink + passed)
    return sizes[jax.random.permutation(jax.random.fold_in(own_key, 2), number_of)]


def noise(rng, extent, scale, reach, cuts=(), kind=jnp.bfloat16):
    array = scale * jax.random.normal(rng, extent, jnp.float32)
    if cuts:
        array = array * block_scale(rng, extent, cuts, -0.22, 0.18)
    return jnp.clip(array, -reach, reach).astype(kind)


def setup_inputs(seed: int = 0) -> dict:
    keys = jax.random.split(jax.random.key(seed), 13)
    tokens = noise(keys[0], (TOKENS, MODEL_WIDTH), 1.0, 6.0, ((0, 32),))
    block_ids = jax.vmap(lambda own: jnp.searchsorted(jnp.cumsum(ragged(own, BLOCKS, SEQ_LEN, BLOCK, 0)), jnp.arange(SEQ_LEN), side="right"))(jax.random.split(keys[1], SEQS)).reshape((SEQS, SEQ_LEN)).astype(jnp.int32)
    query_weight = noise(keys[2], (MODEL_WIDTH, QUERY_HEADS * HEAD_WIDTH), 0.08, 0.47851562, ((0, 16),))
    key_projection_weight = noise(keys[3], (MODEL_WIDTH, KEY_VALUE_HEADS * HEAD_WIDTH), 0.08, 0.47851562, ((0, 16),))
    value_projection_weight = noise(keys[4], (MODEL_WIDTH, KEY_VALUE_HEADS * HEAD_WIDTH), MODEL_WIDTH ** -0.5, 0.125, ((0, 16),))
    output_weight = noise(keys[5], (QUERY_HEADS * HEAD_WIDTH, MODEL_WIDTH), 0.4, 2.390625, ((0, 16),))
    gate_weight = noise(keys[6], (MODEL_WIDTH, FF), MODEL_WIDTH ** -0.5, 0.125, ((0, 16),))
    up_weight = noise(keys[7], (MODEL_WIDTH, FF), MODEL_WIDTH ** -0.5, 0.125, ((0, 16),))
    down_weight = noise(keys[8], (FF, MODEL_WIDTH), 0.06, 0.359375, ((0, 16),))
    attn_gain = jnp.clip(1.0 + 0.1 * jax.random.normal(keys[9], (MODEL_WIDTH,), jnp.float32), 0.5, 1.5).astype(jnp.bfloat16)
    mlp_gain = jnp.clip(1.0 + 0.1 * jax.random.normal(keys[10], (MODEL_WIDTH,), jnp.float32), 0.5, 1.5).astype(jnp.bfloat16)
    cotangent = noise(keys[11], (TOKENS, MODEL_WIDTH), 1.0, 6.0, ((0, 32),))
    return dict(tokens=tokens, block_ids=block_ids, query_weight=query_weight, key_projection_weight=key_projection_weight, value_projection_weight=value_projection_weight, output_weight=output_weight, gate_weight=gate_weight, up_weight=up_weight, down_weight=down_weight, attn_gain=attn_gain, mlp_gain=mlp_gain, cotangent=cotangent)


NORM_EPS = 1e-05
RESIDUAL = 0.22
SCORE_SCALE = 0.015625
ROPE_THETA = 10000000.0
HIGHEST = lax.Precision.HIGHEST

@jax.custom_vjp
def reduced_precision(v):
    return lax.optimization_barrier(v.astype(jnp.bfloat16)).astype(jnp.float32)

@jax.custom_vjp
def reduced_backward(v):
    return v

def low_keep(v):
    return (reduced_precision(v), None)

def low_pass(kept, grad):
    return (grad,)

def back_keep(v):
    return (v, None)

def back_low(kept, grad):
    return (reduced_precision(grad),)
reduced_precision.defvjp(low_keep, low_pass)
reduced_backward.defvjp(back_keep, back_low)

def rope_tables(token_length, width):
    half_width = width // 2
    frequency = ROPE_THETA ** (-(jnp.arange(half_width, dtype=jnp.float32) * 2.0) / width)
    angles = jnp.arange(token_length, dtype=jnp.float32)[:, None] * frequency[None, :]
    cosine_table = jnp.concatenate([jnp.cos(angles), jnp.cos(angles)], axis=1)
    sine_table = jnp.concatenate([jnp.sin(angles), jnp.sin(angles)], axis=1)
    return (cosine_table, sine_table)

def apply_rotary(value_rows, cosine_table, sine_table):
    half_width = value_rows.shape[-1] // 2
    turned = jnp.concatenate([-value_rows[..., half_width:], value_rows[..., :half_width]], axis=-1)
    return value_rows * cosine_table[:, None, :] + turned * sine_table[:, None, :]

def rms_norm(value_rows, gain_vec):
    return value_rows * lax.rsqrt(lax.optimization_barrier(jnp.mean(value_rows * value_rows, axis=-1, keepdims=True)) + NORM_EPS) * gain_vec

def matrix_multiply(left_side, right_side):
    return jnp.dot(left_side, right_side, precision=HIGHEST)

def one_sequence(params, inputs, seq_ids):
    query_w, key_matrix, value_matrix, output_w, gate_w, up_w, down_w, attn_g, mlp_g = params
    token_length = inputs.shape[0]
    heads_per_group = QUERY_HEADS // KEY_VALUE_HEADS
    cosine_table, sine_table = rope_tables(token_length, HEAD_WIDTH)
    first_normed = reduced_precision(rms_norm(inputs, attn_g))
    query_rows = reduced_precision(apply_rotary(reduced_backward(matrix_multiply(first_normed, query_w)).reshape(token_length, QUERY_HEADS, HEAD_WIDTH), cosine_table, sine_table))
    keys_rotated = reduced_precision(apply_rotary(reduced_backward(matrix_multiply(first_normed, key_matrix)).reshape(token_length, KEY_VALUE_HEADS, HEAD_WIDTH), cosine_table, sine_table))
    value_rows = reduced_backward(reduced_precision(matrix_multiply(first_normed, value_matrix))).reshape(token_length, KEY_VALUE_HEADS, HEAD_WIDTH)
    grouped_heads = query_rows.reshape(token_length, KEY_VALUE_HEADS, heads_per_group, HEAD_WIDTH)
    scores = reduced_backward(SCORE_SCALE * jnp.einsum('qhgd,thd->hgqt', grouped_heads, keys_rotated, precision=HIGHEST))
    visible = seq_ids[None, :] <= seq_ids[:, None]
    scores = jnp.where(visible[None, None], scores, -1e+30)
    attend = jax.nn.softmax(scores, axis=-1)
    mixed = jnp.einsum('hgqt,thd->qhgd', reduced_precision(attend), value_rows, precision=HIGHEST).reshape(token_length, QUERY_HEADS * HEAD_WIDTH)
    mixed = reduced_backward(reduced_precision(mixed))
    residual = inputs + RESIDUAL * reduced_backward(matrix_multiply(mixed, output_w))
    normed2 = reduced_precision(rms_norm(residual, mlp_g))
    gating = reduced_backward(matrix_multiply(normed2, gate_w))
    upward = reduced_backward(matrix_multiply(normed2, up_w))
    hidden = reduced_precision(jax.nn.silu(gating) * upward)
    return residual + RESIDUAL * reduced_backward(matrix_multiply(hidden, down_w))

def reference(tokens, block_ids, query_weight, key_projection_weight, value_projection_weight, output_weight, gate_weight, up_weight, down_weight, attn_gain, mlp_gain, cotangent):
    params = tuple((weight.astype(jnp.float32) for weight in (query_weight, key_projection_weight, value_projection_weight, output_weight, gate_weight, up_weight, down_weight, attn_gain, mlp_gain)))
    sequences = tokens.astype(jnp.float32).reshape(SEQS, SEQ_LEN, MODEL_WIDTH)

    def forward(param_set, seq_inputs):

        def scan_step(scan_carry, scan_item):
            return (scan_carry, jax.checkpoint(one_sequence)(param_set, scan_item[0], scan_item[1]))
        _, outputs_all = lax.scan(scan_step, None, (seq_inputs, block_ids))
        return outputs_all
    outputs_all, pullback = jax.vjp(forward, params, sequences)
    weight_grads, seq_grads = pullback(cotangent.astype(jnp.float32).reshape(SEQS, SEQ_LEN, MODEL_WIDTH))
    return (outputs_all.reshape(TOKENS, MODEL_WIDTH).astype(jnp.bfloat16), seq_grads.reshape(TOKENS, MODEL_WIDTH), weight_grads[0], weight_grads[1], weight_grads[2], weight_grads[3], weight_grads[4], weight_grads[5], weight_grads[6], weight_grads[7], weight_grads[8])
```

```python
import jax
import jax.numpy as jnp
from jax import lax
from jax.sharding import Mesh
from jax.sharding import PartitionSpec as P

QUERY_HEADS = 32
KEY_VALUE_HEADS = 8
HEAD_WIDTH = 64


NORM_EPS = 1e-05
RESIDUAL = 0.22
SCORE_SCALE = 0.015625
ROPE_THETA = 10000000.0


def rope_tables(token_length, width):
    half_width = width // 2
    frequency = ROPE_THETA ** (-(jnp.arange(half_width, dtype=jnp.float32) * 2.0) / width)
    angles = jnp.arange(token_length, dtype=jnp.float32)[:, None] * frequency[None, :]
    cosine_table = jnp.concatenate([jnp.cos(angles), jnp.cos(angles)], axis=1)
    sine_table = jnp.concatenate([jnp.sin(angles), jnp.sin(angles)], axis=1)
    return (cosine_table, sine_table)


def apply_rotary(value_rows, cosine_table, sine_table):
    half_width = value_rows.shape[-1] // 2
    turned = jnp.concatenate([-value_rows[..., half_width:], value_rows[..., :half_width]], axis=-1)
    return value_rows * cosine_table[:, None, :] + turned * sine_table[:, None, :]


def rms_norm(value_rows, gain_vec):
    return (
        value_rows
        * lax.rsqrt(jnp.mean(value_rows * value_rows, axis=-1, keepdims=True) + NORM_EPS)
        * gain_vec
    )


def matrix_product(left_side, right_side):
    return jnp.dot(left_side, right_side, preferred_element_type=jnp.float32)


def contract_rows(left_side, right_side):
    return lax.dot_general(
        left_side, right_side, (((0,), (0,)), ((), ())), preferred_element_type=jnp.float32
    )


def contract_cols(left_side, right_side):
    return lax.dot_general(
        left_side, right_side, (((1,), (1,)), ((), ())), preferred_element_type=jnp.float32
    )


TENSOR = ("replica", "chip", "core")
INNER = ("chip", "core")
GROUP = ("slow", "chip", "core")


def gather_tokens(rows):
    return lax.all_gather(rows, TENSOR, axis=0, tiled=True)


def scatter_tokens(partial):
    return lax.psum_scatter(partial, TENSOR, scatter_dimension=0, tiled=True)


def take_half(array, axis, replicas):
    part = lax.axis_index("replica")
    return lax.dynamic_index_in_dim(array, part, axis, keepdims=False)


def shards(
    tokens,
    block_ids,
    query_weight,
    key_projection_weight,
    value_projection_weight,
    output_weight,
    gate_weight,
    up_weight,
    down_weight,
    attn_gain,
    mlp_gain,
    cotangent,
):
    token_length, width = tokens.shape
    row_count, hidden_width = gate_weight.shape
    replicas = lax.axis_size("replica")
    slow = lax.axis_size("slow")
    inner = lax.axis_size("chip") * lax.axis_size("core")
    unit = hidden_width // (slow * inner * replicas)
    local_hidden = slow * unit
    heads_per_group = QUERY_HEADS // KEY_VALUE_HEADS
    group_width = heads_per_group * HEAD_WIDTH
    query_width = query_weight.shape[1]
    key_width = key_projection_weight.shape[1]
    lanes = 128

    gain_columns = jnp.pad(
        jnp.stack([attn_gain, mlp_gain], axis=1), ((0, 0), (0, lanes - 2))
    )
    qkv_local = jnp.concatenate(
        [query_weight, key_projection_weight, value_projection_weight, gain_columns], axis=1
    )
    qkv_all = lax.all_gather(qkv_local, GROUP, axis=0, tiled=True)
    output_all = lax.all_gather(output_weight, GROUP, axis=0, tiled=True)

    def column_slices(weight):
        mine = take_half(weight.reshape(row_count, slow, inner, replicas, unit), 3, replicas)
        return mine.transpose(2, 0, 1, 3)

    both = jnp.stack([column_slices(gate_weight), column_slices(up_weight)], axis=2)
    both = lax.all_to_all(both, INNER, split_axis=0, concat_axis=0, tiled=True)
    wide_local = both.reshape(inner * row_count, 2 * local_hidden)
    down_local = take_half(down_weight.reshape(replicas, unit, width), 0, replicas)
    wide_all = lax.all_gather(wide_local, "slow", axis=0, tiled=True)
    down_all = lax.all_gather(down_local, "slow", axis=0, tiled=True)

    gains = qkv_all[:, query_width + 2 * key_width :][:, :2].T.astype(jnp.float32)
    attn_scale, mlp_scale = gains[0], gains[1]
    inputs = tokens.astype(jnp.float32)
    seq_ids = block_ids[0]
    visible = seq_ids[None, :] <= seq_ids[:, None]
    cosine_table, sine_table = rope_tables(token_length, HEAD_WIDTH)

    def rotary_flat(flat_projection, head_count):
        return apply_rotary(
            flat_projection.reshape(token_length, head_count, HEAD_WIDTH), cosine_table, sine_table
        ).reshape(token_length, head_count * HEAD_WIDTH)

    first_normed = rms_norm(inputs, attn_scale).astype(jnp.bfloat16)
    projected = matrix_product(first_normed, qkv_all)
    query_rows = rotary_flat(projected[:, :query_width], QUERY_HEADS).astype(jnp.bfloat16)
    keys_rotated = rotary_flat(
        projected[:, query_width : query_width + key_width], KEY_VALUE_HEADS
    ).astype(jnp.bfloat16)
    value_rows = projected[:, query_width + key_width : query_width + 2 * key_width].astype(
        jnp.bfloat16
    )

    def group_parts(head_cluster):
        query_part = query_rows[
            :, head_cluster * group_width : (head_cluster + 1) * group_width
        ].reshape(token_length, heads_per_group, HEAD_WIDTH)
        key_part = keys_rotated[:, head_cluster * HEAD_WIDTH : (head_cluster + 1) * HEAD_WIDTH]
        value_part = value_rows[:, head_cluster * HEAD_WIDTH : (head_cluster + 1) * HEAD_WIDTH]
        scores = SCORE_SCALE * jnp.einsum(
            "qgd,td->gqt", query_part, key_part, preferred_element_type=jnp.float32
        )
        scores = jnp.where(visible[None], scores, -1e30)
        return (query_part, key_part, value_part, scores)

    mixed_parts = []
    logsum_parts = []
    for head_cluster in range(KEY_VALUE_HEADS):
        query_part, key_part, value_part, scores = group_parts(head_cluster)
        row_max = jnp.max(scores, axis=-1, keepdims=True)
        logsum = row_max + jnp.log(jnp.sum(jnp.exp(scores - row_max), axis=-1, keepdims=True))
        attend = jnp.exp(scores - logsum).astype(jnp.bfloat16)
        mixed_parts.append(
            jnp.einsum(
                "gqt,td->qgd", attend, value_part, preferred_element_type=jnp.float32
            ).reshape(token_length, group_width)
        )
        logsum_parts.append(logsum)
    mixed = jnp.concatenate(mixed_parts, axis=1).astype(jnp.bfloat16)
    residual = inputs + RESIDUAL * matrix_product(mixed, output_all)
    normed2 = rms_norm(residual, mlp_scale).astype(jnp.bfloat16)
    grad_out = cotangent.astype(jnp.float32)
    down_in = (RESIDUAL * grad_out).astype(jnp.bfloat16)
    down_in_all = gather_tokens(down_in)
    normed2_all = gather_tokens(normed2)
    wide = matrix_product(normed2_all, wide_all)
    gating, upward = wide[:, :local_hidden], wide[:, local_hidden:]
    hidden_act = (jax.nn.silu(gating) * upward).astype(jnp.bfloat16)
    mlp_out = scatter_tokens(matrix_product(hidden_act, down_all).astype(jnp.bfloat16))
    output = (residual + RESIDUAL * mlp_out.astype(jnp.float32)).astype(jnp.bfloat16)

    hidden_grad = contract_cols(down_in_all, down_all)
    grad_down = contract_rows(hidden_act, down_in_all).astype(jnp.bfloat16)
    down_part = lax.psum_scatter(grad_down, "slow", scatter_dimension=0, tiled=True)
    _, swiglu_pull = jax.vjp(lambda first, second: jax.nn.silu(first) * second, gating, upward)
    gating_grad, upward_grad = swiglu_pull(hidden_grad)
    wide_in = jnp.concatenate(
        [gating_grad.astype(jnp.bfloat16), upward_grad.astype(jnp.bfloat16)], axis=1
    )
    normed2_grad = scatter_tokens(contract_cols(wide_in, wide_all).astype(jnp.bfloat16)).astype(
        jnp.float32
    )
    grad_wide = contract_rows(normed2_all, wide_in).astype(jnp.bfloat16)
    wide_part = lax.psum_scatter(grad_wide, "slow", scatter_dimension=0, tiled=True)
    wide_part = lax.all_to_all(
        wide_part.reshape(inner, row_count, 2, slow, unit),
        INNER,
        split_axis=0,
        concat_axis=0,
        tiled=True,
    )
    wide_full = lax.all_gather(wide_part, "replica", axis=0, tiled=False)
    wide_full = wide_full.transpose(3, 2, 4, 1, 0, 5).reshape(2, row_count, hidden_width)
    gate_shard = wide_full[0].astype(jnp.float32)
    up_shard = wide_full[1].astype(jnp.float32)
    down_shard = lax.all_gather(down_part, "replica", axis=0, tiled=True).astype(jnp.float32)

    _, norm2_pull = jax.vjp(rms_norm, residual, mlp_scale)
    residual_part, grad_mlp_gain = norm2_pull(normed2_grad)
    residual_grad = grad_out + residual_part
    attn_in = (RESIDUAL * residual_grad).astype(jnp.bfloat16)
    grad_output = contract_rows(mixed, attn_in)
    mixed_grad = contract_cols(attn_in, output_all).astype(jnp.bfloat16)
    query_grads = []
    key_grads = []
    value_grads = []
    for head_cluster in range(KEY_VALUE_HEADS):
        query_part, key_part, value_part, scores = group_parts(head_cluster)
        attend = jnp.exp(scores - logsum_parts[head_cluster])
        grad_part = mixed_grad[
            :, head_cluster * group_width : (head_cluster + 1) * group_width
        ].reshape(token_length, heads_per_group, HEAD_WIDTH)
        attend_grad = jnp.einsum(
            "qgd,td->gqt", grad_part, value_part, preferred_element_type=jnp.float32
        )
        row_delta = jnp.sum(attend * attend_grad, axis=-1, keepdims=True)
        score_grad = (attend * (attend_grad - row_delta)).astype(jnp.bfloat16)
        query_grads.append(
            (
                SCORE_SCALE
                * jnp.einsum(
                    "gqt,td->qgd", score_grad, key_part, preferred_element_type=jnp.float32
                )
            ).reshape(token_length, group_width)
        )
        key_grads.append(
            SCORE_SCALE
            * jnp.einsum("gqt,qgd->td", score_grad, query_part, preferred_element_type=jnp.float32)
        )
        value_grads.append(
            jnp.einsum(
                "gqt,qgd->td",
                attend.astype(jnp.bfloat16),
                grad_part,
                preferred_element_type=jnp.float32,
            )
        )
    queries_grad = jnp.concatenate(query_grads, axis=1)
    keys_grad = jnp.concatenate(key_grads, axis=1)
    value_lin_grad = jnp.concatenate(value_grads, axis=1).astype(jnp.bfloat16)
    _, query_rope_pull = jax.vjp(
        lambda flat_projection: rotary_flat(flat_projection, QUERY_HEADS),
        jnp.zeros((token_length, QUERY_HEADS * HEAD_WIDTH), jnp.float32),
    )
    _, key_rope_pull = jax.vjp(
        lambda flat_projection: rotary_flat(flat_projection, KEY_VALUE_HEADS),
        jnp.zeros((token_length, KEY_VALUE_HEADS * HEAD_WIDTH), jnp.float32),
    )
    query_lin_grad = query_rope_pull(queries_grad)[0].astype(jnp.bfloat16)
    key_lin_grad = key_rope_pull(keys_grad)[0].astype(jnp.bfloat16)
    qkv_in = jnp.concatenate(
        [
            query_lin_grad,
            key_lin_grad,
            value_lin_grad,
            jnp.zeros((token_length, lanes), jnp.bfloat16),
        ],
        axis=1,
    )
    grad_qkv = contract_rows(first_normed, qkv_in).astype(jnp.bfloat16)
    normed1_grad = contract_cols(qkv_in, qkv_all)
    _, norm1_pull = jax.vjp(rms_norm, inputs, attn_scale)
    input_part, grad_attn_gain = norm1_pull(normed1_grad)
    input_grad = residual_grad + input_part
    gain_grads = jnp.stack([grad_attn_gain, grad_mlp_gain], axis=1).astype(jnp.bfloat16)
    grad_qkv = lax.dynamic_update_slice(
        grad_qkv, gain_grads, (0, query_width + 2 * key_width)
    )
    output_shard = lax.psum_scatter(
        grad_output.astype(jnp.bfloat16), GROUP, scatter_dimension=0, tiled=True
    )
    qkv_shard = lax.psum_scatter(grad_qkv, GROUP, scatter_dimension=0, tiled=True)

    def replica_sum(part):
        total = part.astype(jnp.float32)
        for shift in range(1, replicas):
            pairs = [(i, (i + shift) % replicas) for i in range(replicas)]
            total = total + lax.ppermute(part, "replica", pairs).astype(jnp.float32)
        return total

    output_shard = replica_sum(output_shard)
    qkv_shard = replica_sum(qkv_shard)
    query_shard = qkv_shard[:, :query_width]
    key_shard = qkv_shard[:, query_width : query_width + key_width]
    value_shard = qkv_shard[:, query_width + key_width : query_width + 2 * key_width]
    attn_gain_shard = qkv_shard[:, query_width + 2 * key_width]
    mlp_gain_shard = qkv_shard[:, query_width + 2 * key_width + 1]
    return (
        output,
        input_grad,
        query_shard,
        key_shard,
        value_shard,
        output_shard,
        gate_shard,
        up_shard,
        down_shard,
        attn_gain_shard,
        mlp_gain_shard,
    )


def solution(mesh):
    replicas, shard_count = mesh.shape["replica"], mesh.shape["shard"]
    inner = KEY_VALUE_HEADS // replicas
    cores = 2
    split_mesh = Mesh(
        mesh.devices.reshape(replicas, shard_count // inner, inner // cores, cores),
        ("replica", "slow", "chip", "core"),
    )
    everyone = P(("replica", "slow", "chip", "core"), None)
    sharded = P(GROUP, None)
    vector = P(GROUP)
    return jax.shard_map(
        shards,
        mesh=split_mesh,
        in_specs=(everyone, everyone) + (sharded,) * 7 + (vector, vector, everyone),
        out_specs=(everyone, everyone) + (sharded,) * 7 + (vector, vector),
        check_vma=False,
    )
```

```python
import jax
import jax.numpy as jnp
from jax import lax
from jax.experimental import pallas as pl
from jax.experimental.pallas import tpu as pltpu
from jax.sharding import Mesh
from jax.sharding import PartitionSpec as P


QUERY_HEADS = 32
KEY_VALUE_HEADS = 8
HEAD_WIDTH = 64


NORM_EPS = 1e-05
RESIDUAL = 0.22
SCORE_SCALE = 0.015625
ROPE_THETA = 10000000.0


def rope_tables(token_length, width):
    half_width = width // 2
    frequency = ROPE_THETA ** (-(jnp.arange(half_width, dtype=jnp.float32) * 2.0) / width)
    angles = jnp.arange(token_length, dtype=jnp.float32)[:, None] * frequency[None, :]
    cosine_table = jnp.concatenate([jnp.cos(angles), jnp.cos(angles)], axis=1)
    sine_table = jnp.concatenate([jnp.sin(angles), jnp.sin(angles)], axis=1)
    return (cosine_table, sine_table)


def rms_norm(value_rows, gain_vec):
    return (
        value_rows
        * lax.rsqrt(jnp.mean(value_rows * value_rows, axis=-1, keepdims=True) + NORM_EPS)
        * gain_vec
    )


def matrix_product(left_side, right_side):
    return jnp.dot(left_side, right_side, preferred_element_type=jnp.float32)


def contract_rows(left_side, right_side):
    return lax.dot_general(
        left_side, right_side, (((0,), (0,)), ((), ())), preferred_element_type=jnp.float32
    )


def contract_cols(left_side, right_side):
    return lax.dot_general(
        left_side, right_side, (((1,), (1,)), ((), ())), preferred_element_type=jnp.float32
    )


GROUP = ("slow", "chip", "core")
LANES = 128


def swap(value, axis):
    return lax.ppermute(value, axis, [(0, 1), (1, 0)])


def order(first_is_zero, one, other):
    return jnp.where(first_is_zero, one, other), jnp.where(first_is_zero, other, one)


def add_parts(*parts):
    total = parts[0].astype(jnp.float32)
    for part in parts[1:]:
        total = total + part.astype(jnp.float32)
    return total


def gather_tokens(rows):
    half = rows.shape[0] // 2
    beside = swap(rows, "chip")
    across = swap(rows, "replica")
    corner_low = swap(beside[:half], "replica")
    corner_high = swap(across[half:], "chip")
    plane = [rows, beside, across, corner_low, corner_high]
    return plane, [swap(part, "core") for part in plane]


def narrow(value):
    return value.astype(jnp.bfloat16)


def scatter_pieces(mine, partner):
    partner = [swap(part, "core") for part in partner]
    own, beside, across, corner = (
        add_parts(keep, send) for keep, send in zip(mine, partner, strict=True)
    )
    half = own.shape[0] // 2
    corner = narrow(corner)
    beside_low = swap(narrow(beside[:half]), "chip")
    across_high = swap(narrow(across[half:]), "replica")
    corner_low = swap(corner[:half], "chip")
    corner_high = swap(corner[half:], "replica")
    across_low = narrow(add_parts(narrow(across[:half]), corner_low))
    beside_high = narrow(add_parts(narrow(beside[half:]), corner_high))
    across_low = swap(across_low, "replica")
    beside_high = swap(beside_high, "chip")
    return jnp.concatenate(
        [
            add_parts(own[:half], beside_low, across_low),
            add_parts(own[half:], across_high, beside_high),
        ],
        axis=0,
    )


def gather_weight(weight):
    return lax.all_gather(weight, GROUP, axis=0, tiled=True)


def turned_lanes(value):
    lane = lax.broadcasted_iota(jnp.int32, value.shape, 1) % HEAD_WIDTH
    half = HEAD_WIDTH // 2
    return jnp.where(
        lane < half,
        pltpu.roll(value, LANES - half, 1),
        pltpu.roll(value, half, 1),
    )


def rotate_lanes(value, cosine, sine, sign):
    columns = []
    for start in range(0, value.shape[1], LANES):
        part = value[:, start : start + LANES]
        columns.append(part * cosine + sign * (turned_lanes(part) * sine))
    return columns[0] if len(columns) == 1 else jnp.concatenate(columns, axis=1)


def cross_dot(left_side, right_side):
    return lax.dot_general(
        left_side, right_side, (((1,), (1,)), ((), ())), preferred_element_type=jnp.float32
    )


def set_bias(bias, key_ids, query_ids):
    @pl.when(pl.program_id(0) == 0)
    def _():
        bias[...] = jnp.where(key_ids[...] <= query_ids[...], 0.0, -1e30)


def attend_forward(
    query, key, value, cosine, sine, key_ids, query_ids, query_out, key_out, value_out, mixed_out,
    logsum_out, bias,
):
    set_bias(bias, key_ids, query_ids)
    rotated = rotate_lanes(query[...], cosine[...], sine[...], 1.0)
    query_out[...] = (rotated.astype(jnp.bfloat16).astype(jnp.float32) * SCORE_SCALE).astype(
        jnp.bfloat16
    )
    key_out[...] = rotate_lanes(key[...], cosine[...], sine[...], 1.0).astype(jnp.bfloat16)
    value_out[...] = value[...].astype(jnp.bfloat16)
    turned_values = value[...].T.astype(jnp.bfloat16)
    heads = query.shape[1] // HEAD_WIDTH
    share = heads * HEAD_WIDTH // key.shape[1]
    outputs = []
    for head in range(heads):
        lanes = slice(head * HEAD_WIDTH, (head + 1) * HEAD_WIDTH)
        group = slice(head // share * HEAD_WIDTH, (head // share + 1) * HEAD_WIDTH)
        scores = cross_dot(key_out[:, group], query_out[:, lanes]) + bias[...]
        top = jnp.max(scores, axis=0, keepdims=True)
        weights = jnp.exp(scores - top)
        total = jnp.sum(weights, axis=0, keepdims=True)
        logsum_out[head : head + 1, :] = top + jnp.log(total)
        attend = (weights * (1.0 / total)).astype(jnp.bfloat16)
        outputs.append(
            jnp.dot(turned_values[group], attend, preferred_element_type=jnp.float32)
        )
    mixed_out[...] = jnp.concatenate(outputs, axis=0).T.astype(jnp.bfloat16)


def attend_backward(
    query, key, value, mixed_grad, logsum, cosine, sine, key_ids, query_ids, query_out, key_out,
    value_out, bias,
):
    set_bias(bias, key_ids, query_ids)
    heads = query.shape[1] // HEAD_WIDTH
    groups = key.shape[1] // HEAD_WIDTH
    share = heads // groups
    turned_keys = key[...].astype(jnp.float32).T.astype(jnp.bfloat16)
    query_grads = []
    key_grads = []
    value_grads = []
    for group_index in range(groups):
        group = slice(group_index * HEAD_WIDTH, (group_index + 1) * HEAD_WIDTH)
        key_grad = value_grad = None
        for head in range(group_index * share, (group_index + 1) * share):
            lanes = slice(head * HEAD_WIDTH, (head + 1) * HEAD_WIDTH)
            scores = cross_dot(key[:, group], query[:, lanes]) + bias[...]
            attend = jnp.exp(scores - logsum[head : head + 1, :])
            attend_grad = cross_dot(value[:, group], mixed_grad[:, lanes])
            delta = jnp.sum(attend * attend_grad, axis=0, keepdims=True)
            score_grad = (attend * (attend_grad - delta)).astype(jnp.bfloat16)
            value_term = matrix_product(attend.astype(jnp.bfloat16), mixed_grad[:, lanes])
            key_term = matrix_product(score_grad, query[:, lanes])
            value_grad = value_term if value_grad is None else value_grad + value_term
            key_grad = key_term if key_grad is None else key_grad + key_term
            query_grads.append(matrix_product(turned_keys[group], score_grad))
        key_grads.append(key_grad)
        value_grads.append(value_grad)
    query_grad = SCORE_SCALE * jnp.concatenate(query_grads, axis=0).T
    key_grad = jnp.concatenate(key_grads, axis=1)
    query_out[...] = rotate_lanes(query_grad, cosine[...], sine[...], -1.0).astype(jnp.bfloat16)
    key_out[...] = rotate_lanes(key_grad, cosine[...], sine[...], -1.0).astype(jnp.bfloat16)
    value_out[...] = jnp.concatenate(value_grads, axis=1).astype(jnp.bfloat16)


def hidden_backward(wide, grads, down, wide_out):
    hidden = down.shape[0]
    hidden_grad = cross_dot(grads[...], down[...])
    gating, upward = wide[:, :hidden], wide[:, hidden:]
    gate = 1.0 / (1.0 + jnp.exp(-gating))
    active = gating * gate
    wide_out[:, :hidden] = (hidden_grad * upward * (gate + active * (1.0 - gate))).astype(
        jnp.bfloat16
    )
    wide_out[:, hidden:] = (hidden_grad * active).astype(jnp.bfloat16)


def hidden_backward_call(wide, grads, down):
    rows, both = wide.shape
    width = grads.shape[1]
    block = 512

    def rows_of(columns):
        return pl.BlockSpec((block, columns), lambda step: (step, 0))

    return pl.pallas_call(
        hidden_backward,
        grid=(rows // block,),
        in_specs=[
            rows_of(both),
            rows_of(width),
            pl.BlockSpec(down.shape, lambda step: (0, 0)),
        ],
        out_specs=rows_of(both),
        out_shape=jax.ShapeDtypeStruct((rows, both), jnp.bfloat16),
        compiler_params=pltpu.CompilerParams(
            dimension_semantics=("arbitrary",), vmem_limit_bytes=56 * 1024 * 1024
        ),
        cost_estimate=pl.CostEstimate(
            flops=rows * both * width,
            bytes_accessed=rows * (both * 6 + width * 2) + down.size * 2,
            transcendentals=rows * both // 2,
        ),
        name="hidden_backward",
    )(wide, grads, down)


def kernel_cost(length, passes):
    return pl.CostEstimate(
        flops=2 * passes * QUERY_HEADS * HEAD_WIDTH * length * length,
        bytes_accessed=12 * length * QUERY_HEADS * HEAD_WIDTH,
        transcendentals=QUERY_HEADS * length * length,
    )


def attention_calls(length):
    step_keys = LANES
    steps = KEY_VALUE_HEADS * HEAD_WIDTH // step_keys
    step_queries = QUERY_HEADS * HEAD_WIDTH // steps
    step_heads = step_queries // HEAD_WIDTH
    key_start = QUERY_HEADS * HEAD_WIDTH // step_keys

    def columns(block, first):
        return pl.BlockSpec((length, block), lambda step: (0, step + first))

    def fixed(*shape):
        return pl.BlockSpec(shape, lambda step: (0, 0))

    tables = [
        fixed(length, LANES),
        fixed(length, LANES),
        fixed(length, 1),
        fixed(1, length),
    ]
    logsum = pl.BlockSpec((step_heads, length), lambda step: (step, 0))
    query_shape = jax.ShapeDtypeStruct((length, QUERY_HEADS * HEAD_WIDTH), jnp.bfloat16)
    key_shape = jax.ShapeDtypeStruct((length, KEY_VALUE_HEADS * HEAD_WIDTH), jnp.bfloat16)
    params = pltpu.CompilerParams(
        dimension_semantics=("arbitrary",), vmem_limit_bytes=48 * 1024 * 1024
    )
    forward = pl.pallas_call(
        attend_forward,
        grid=(steps,),
        in_specs=[
            columns(step_queries, 0),
            columns(step_keys, key_start),
            columns(step_keys, key_start + steps),
            *tables,
        ],
        out_specs=[
            columns(step_queries, 0),
            columns(step_keys, 0),
            columns(step_keys, 0),
            columns(step_queries, 0),
            logsum,
        ],
        out_shape=[
            query_shape,
            key_shape,
            key_shape,
            query_shape,
            jax.ShapeDtypeStruct((QUERY_HEADS, length), jnp.float32),
        ],
        scratch_shapes=[pltpu.VMEM((length, length), jnp.float32)],
        compiler_params=params,
        cost_estimate=kernel_cost(length, 2),
        name="attend_forward",
    )
    backward = pl.pallas_call(
        attend_backward,
        grid=(steps,),
        in_specs=[
            columns(step_queries, 0),
            columns(step_keys, 0),
            columns(step_keys, 0),
            columns(step_queries, 0),
            logsum,
            *tables,
        ],
        out_specs=[columns(step_queries, 0), columns(step_keys, 0), columns(step_keys, 0)],
        out_shape=[query_shape, key_shape, key_shape],
        scratch_shapes=[pltpu.VMEM((length, length), jnp.float32)],
        compiler_params=params,
        cost_estimate=kernel_cost(length, 5),
        name="attend_backward",
    )
    return forward, backward


def layer(
    tokens,
    block_ids,
    query_weight,
    key_projection_weight,
    value_projection_weight,
    output_weight,
    gate_weight,
    up_weight,
    down_weight,
    attn_gain,
    mlp_gain,
    cotangent,
):
    token_length, _ = tokens.shape
    row_count, hidden_width = gate_weight.shape
    slow = lax.axis_size("slow")
    unit = hidden_width // (slow * 8)
    local_hidden = slow * unit
    query_width = query_weight.shape[1]
    key_width = key_projection_weight.shape[1]
    qkv_width = query_width + 2 * key_width
    first_replica = lax.axis_index("replica") == 0
    first_chip = lax.axis_index("chip") == 0
    first_core = lax.axis_index("core") == 0

    gain_columns = jnp.pad(
        jnp.stack([attn_gain, mlp_gain], axis=1), ((0, 0), (0, LANES - 2))
    )
    qkv_local = jnp.concatenate(
        [query_weight, key_projection_weight, value_projection_weight, gain_columns], axis=1
    )
    qkv_all = gather_weight(qkv_local)
    output_all = gather_weight(output_weight)

    def column_slices(weight, member):
        pieces = []
        for step in range(slow):
            start = (step * 4 + member) * 2 * unit
            pieces.append(
                jnp.where(
                    first_replica,
                    weight[:, start : start + unit],
                    weight[:, start + unit : start + 2 * unit],
                )
            )
        return pieces

    packed = [
        jnp.concatenate(
            column_slices(gate_weight, member) + column_slices(up_weight, member), axis=1
        )
        for member in range(4)
    ]
    near, far = order(
        first_chip,
        jnp.concatenate(packed[:2], axis=0),
        jnp.concatenate(packed[2:], axis=0),
    )
    wide_blocks = []
    for block in order(first_chip, near, swap(far, "chip")):
        near, far = order(first_core, block[:row_count], block[row_count:])
        wide_blocks.extend(order(first_core, near, swap(far, "core")))
    wide_local = jnp.concatenate(wide_blocks, axis=0)
    down_local = jnp.where(first_replica, down_weight[:unit], down_weight[unit:])
    wide_all = lax.all_gather(wide_local, "slow", axis=0, tiled=True)
    down_all = lax.all_gather(down_local, "slow", axis=0, tiled=True)

    gains = qkv_all[:, qkv_width:][:, :2].T.astype(jnp.float32)
    attn_scale, mlp_scale = gains[0], gains[1]
    inputs = tokens.astype(jnp.float32)
    cosine_table, sine_table = rope_tables(token_length, HEAD_WIDTH)
    signs = jnp.where(jnp.arange(HEAD_WIDTH) < HEAD_WIDTH // 2, -1.0, 1.0)
    tables = (
        jnp.tile(cosine_table, (1, LANES // HEAD_WIDTH)),
        jnp.tile(sine_table * signs, (1, LANES // HEAD_WIDTH)),
        block_ids.T,
        block_ids,
    )
    attend_forward_call, attend_backward_call = attention_calls(token_length)
    first_normed = rms_norm(inputs, attn_scale).astype(jnp.bfloat16)
    projected = matrix_product(first_normed, qkv_all)
    query_rows, key_rows, value_rows, mixed, logsum = attend_forward_call(
        projected, projected, projected, *tables
    )
    residual = inputs + RESIDUAL * matrix_product(mixed, output_all)
    normed2 = rms_norm(residual, mlp_scale).astype(jnp.bfloat16)
    plane, partners = gather_tokens(normed2)
    normed2_all = jnp.concatenate(plane + partners, axis=0)
    grad_out = cotangent.astype(jnp.float32)
    down_in = (RESIDUAL * grad_out).astype(jnp.bfloat16)
    plane, partners = gather_tokens(down_in)
    down_in_all = jnp.concatenate(plane + partners, axis=0)
    wide = matrix_product(normed2_all, wide_all)
    gating, upward = wide[:, :local_hidden], wide[:, local_hidden:]
    hidden_act = (jax.nn.silu(gating) * upward).astype(jnp.bfloat16)
    grad_down = narrow(contract_rows(hidden_act, down_in_all))
    down_part = lax.psum_scatter(grad_down, "slow", scatter_dimension=0, tiled=True)

    def pieces_of(plane_rows):
        return [plane_rows[i * token_length : (i + 1) * token_length] for i in range(4)]

    def to_owners(rows, weight, product):
        partner = narrow(product(rows[4 * token_length :], weight))
        mine = narrow(product(rows[: 4 * token_length], weight))
        return scatter_pieces(pieces_of(mine), pieces_of(partner))

    mlp_out = to_owners(hidden_act, down_all, matrix_product)
    output = (residual + RESIDUAL * mlp_out).astype(jnp.bfloat16)
    wide_in = hidden_backward_call(wide, down_in_all, down_all)
    normed2_grad = to_owners(wide_in, wide_all, contract_cols)
    parts = []
    for start in (0, local_hidden):
        grad = narrow(contract_rows(normed2_all, wide_in[:, start : start + local_hidden]))
        parts.append(lax.psum_scatter(grad, "slow", scatter_dimension=0, tiled=True))

    def exchange(part):
        near, far = order(first_chip, part[: 2 * row_count], part[2 * row_count :])
        low, high = order(first_chip, near, swap(far, "chip"))
        members = []
        for block in (low, high):
            near, far = order(first_core, block[:row_count], block[row_count:])
            members.extend(order(first_core, near, swap(far, "core")))
        members = jnp.concatenate(members, axis=0)
        sources = order(first_replica, members, swap(members, "replica"))
        pieces = []
        for step in range(slow):
            for member in range(4):
                for source in sources:
                    pieces.append(
                        source[
                            member * row_count : (member + 1) * row_count,
                            step * unit : (step + 1) * unit,
                        ]
                    )
        return jnp.concatenate(pieces, axis=1).astype(jnp.float32)

    gate_shard, up_shard = exchange(parts[0]), exchange(parts[1])
    down_shard = jnp.concatenate(
        order(first_replica, down_part, swap(down_part, "replica")), axis=0
    ).astype(jnp.float32)

    _, norm2_pull = jax.vjp(rms_norm, residual, mlp_scale)
    residual_part, grad_mlp_gain = norm2_pull(normed2_grad)
    residual_grad = grad_out + residual_part

    def member_columns(left):
        blocks = {}
        for chip in range(2):
            for core in range(2):
                blocks[chip, core] = jnp.concatenate(
                    [
                        left[:, start : start + row_count]
                        for start in (
                            (step * 4 + chip * 2 + core) * row_count for step in range(slow)
                        )
                    ],
                    axis=1,
                )
        near = [order(first_chip, blocks[0, core], blocks[1, core]) for core in range(2)]
        chips = [order(first_core, near[0][chip], near[1][chip]) for chip in range(2)]
        return [[chips[chip][core] for chip in range(2)] for core in range(2)]

    def weight_part(left, right):
        half = right.shape[1] // 2
        sides = order(first_replica, right[:, :half], right[:, half:])
        blocks = member_columns(left)
        products = []
        for chips in (blocks[1], blocks[0]):
            products.append(
                [
                    narrow(contract_rows(chips[chip], sides[side]))
                    for side, chip in ((0, 0), (0, 1), (1, 0), (1, 1))
                ]
            )
        partner, mine = products
        return narrow(scatter_pieces(mine, partner))

    def both_sides(part):
        return jnp.concatenate(
            order(first_replica, part, swap(part, "replica")), axis=1
        ).astype(jnp.float32)

    attn_in = (RESIDUAL * residual_grad).astype(jnp.bfloat16)
    output_part = weight_part(mixed, attn_in)
    output_part = lax.psum_scatter(output_part, "slow", scatter_dimension=0, tiled=True)
    output_shard = both_sides(output_part)
    mixed_grad = contract_cols(attn_in, output_all).astype(jnp.bfloat16)
    query_lin_grad, key_lin_grad, value_lin_grad = attend_backward_call(
        query_rows, key_rows, value_rows, mixed_grad, logsum, *tables
    )
    qkv_in = jnp.concatenate([query_lin_grad, key_lin_grad, value_lin_grad], axis=1)
    qkv_sum = weight_part(first_normed, qkv_in)
    normed1_grad = contract_cols(qkv_in, qkv_all[:, :qkv_width])
    _, norm1_pull = jax.vjp(rms_norm, inputs, attn_scale)
    input_part, grad_attn_gain = norm1_pull(normed1_grad)
    input_grad = residual_grad + input_part
    gain_grads = jnp.stack([grad_attn_gain, grad_mlp_gain], axis=0)
    for axis in ("core", "chip", "replica"):
        gain_grads = gain_grads + swap(gain_grads, axis)
    gain_rows = jnp.pad(member_columns(gain_grads)[0][0].T, ((0, 0), (0, LANES - 2)))
    qkv_sum = jnp.concatenate([qkv_sum, gain_rows.astype(jnp.bfloat16)], axis=1)
    qkv_part = lax.psum_scatter(qkv_sum, "slow", scatter_dimension=0, tiled=True)
    qkv_shard = both_sides(qkv_part[:, : qkv_width // 2])
    attn_gain_shard = qkv_part[:, qkv_width // 2].astype(jnp.float32)
    mlp_gain_shard = qkv_part[:, qkv_width // 2 + 1].astype(jnp.float32)
    return (
        output,
        input_grad,
        qkv_shard[:, :query_width],
        qkv_shard[:, query_width : query_width + key_width],
        qkv_shard[:, query_width + key_width :],
        output_shard,
        gate_shard,
        up_shard,
        down_shard,
        attn_gain_shard,
        mlp_gain_shard,
    )


def solution(mesh):
    replicas, shard_count = mesh.shape["replica"], mesh.shape["shard"]
    inner = KEY_VALUE_HEADS // replicas
    cores = 2
    split_mesh = Mesh(
        mesh.devices.reshape(replicas, shard_count // inner, inner // cores, cores),
        ("replica", "slow", "chip", "core"),
    )
    everyone = P(("replica", "slow", "chip", "core"), None)
    sharded = P(GROUP, None)
    vector = P(GROUP)
    return jax.shard_map(
        layer,
        mesh=split_mesh,
        in_specs=(everyone, everyone) + (sharded,) * 7 + (vector, vector, everyone),
        out_specs=(everyone, everyone) + (sharded,) * 7 + (vector, vector),
        check_vma=False,
    )
```

```python
import jax
import jax.numpy as jnp
from jax import lax
from jax.experimental import pallas as pl
from jax.experimental.pallas import tpu as pltpu
from jax.sharding import Mesh
from jax.sharding import PartitionSpec as P


QUERY_HEADS = 32
KEY_VALUE_HEADS = 8
HEAD_WIDTH = 64


NORM_EPS = 1e-05
RESIDUAL = 0.22
SCORE_SCALE = 0.015625
ROPE_THETA = 10000000.0


def rope_tables(token_length, width):
    half_width = width // 2
    frequency = ROPE_THETA ** (-(jnp.arange(half_width, dtype=jnp.float32) * 2.0) / width)
    angles = jnp.arange(token_length, dtype=jnp.float32)[:, None] * frequency[None, :]
    cosine_table = jnp.concatenate([jnp.cos(angles), jnp.cos(angles)], axis=1)
    sine_table = jnp.concatenate([jnp.sin(angles), jnp.sin(angles)], axis=1)
    return (cosine_table, sine_table)


def rms_norm(value_rows, gain_vec):
    return (
        value_rows
        * lax.rsqrt(jnp.mean(value_rows * value_rows, axis=-1, keepdims=True) + NORM_EPS)
        * gain_vec
    )


def matrix_product(left_side, right_side):
    return jnp.dot(left_side, right_side, preferred_element_type=jnp.float32)


def contract_rows(left_side, right_side):
    return lax.dot_general(
        left_side, right_side, (((0,), (0,)), ((), ())), preferred_element_type=jnp.float32
    )


def contract_cols(left_side, right_side):
    return lax.dot_general(
        left_side, right_side, (((1,), (1,)), ((), ())), preferred_element_type=jnp.float32
    )


REPLICA_AXIS, SLOW_AXIS, CHIP_AXIS, CORE_AXIS = "replica", "slow", "chip", "core"
GROUP = (SLOW_AXIS, CHIP_AXIS, CORE_AXIS)
LANES = 128


def swap(value, axis):
    return lax.ppermute(value, axis, [(0, 1), (1, 0)])


def order(first_is_zero, one, other):
    return jnp.where(first_is_zero, one, other), jnp.where(first_is_zero, other, one)


def add_parts(*parts):
    total = parts[0].astype(jnp.float32)
    for part in parts[1:]:
        total = total + part.astype(jnp.float32)
    return total


def gather_tokens(rows):
    half = rows.shape[0] // 2
    beside = swap(rows, CHIP_AXIS)
    across = swap(rows, REPLICA_AXIS)
    corner_low = swap(beside[:half], REPLICA_AXIS)
    corner_high = swap(across[half:], CHIP_AXIS)
    plane = [rows, beside, across, corner_low, corner_high]
    return plane, [swap(part, CORE_AXIS) for part in plane]


def narrow(value):
    return value.astype(jnp.bfloat16)


def scatter_pieces(mine, partner):
    partner = [swap(part, CORE_AXIS) for part in partner]
    own, beside, across, corner = (
        add_parts(keep, send) for keep, send in zip(mine, partner, strict=True)
    )
    half = own.shape[0] // 2
    corner = narrow(corner)
    beside_low = swap(narrow(beside[:half]), CHIP_AXIS)
    across_high = swap(narrow(across[half:]), REPLICA_AXIS)
    corner_low = swap(corner[:half], CHIP_AXIS)
    corner_high = swap(corner[half:], REPLICA_AXIS)
    across_low = narrow(add_parts(narrow(across[:half]), corner_low))
    beside_high = narrow(add_parts(narrow(beside[half:]), corner_high))
    across_low = swap(across_low, REPLICA_AXIS)
    beside_high = swap(beside_high, CHIP_AXIS)
    return jnp.concatenate(
        [
            add_parts(own[:half], beside_low, across_low),
            add_parts(own[half:], across_high, beside_high),
        ],
        axis=0,
    )


def gather_weight(weight):
    return lax.all_gather(weight, GROUP, axis=0, tiled=True)


def turned_lanes(value):
    lane = lax.broadcasted_iota(jnp.int32, value.shape, 1) % HEAD_WIDTH
    half = HEAD_WIDTH // 2
    return jnp.where(
        lane < half,
        pltpu.roll(value, LANES - half, 1),
        pltpu.roll(value, half, 1),
    )


def rotate_lanes(value, cosine, sine, sign):
    columns = []
    for start in range(0, value.shape[1], LANES):
        part = value[:, start : start + LANES]
        columns.append(part * cosine + sign * (turned_lanes(part) * sine))
    return columns[0] if len(columns) == 1 else jnp.concatenate(columns, axis=1)


def cross_dot(left_side, right_side):
    return lax.dot_general(
        left_side, right_side, (((1,), (1,)), ((), ())), preferred_element_type=jnp.float32
    )


def set_bias(bias, key_ids, query_ids):
    @pl.when(pl.program_id(0) == 0)
    def _():
        bias[...] = jnp.where(key_ids[...] <= query_ids[...], 0.0, -1e30)


def attend_forward(
    query, key, value, cosine, sine, key_ids, query_ids, query_out, key_out, value_out, mixed_out,
    logsum_out, bias,
):
    set_bias(bias, key_ids, query_ids)
    rotated = rotate_lanes(query[...], cosine[...], sine[...], 1.0)
    query_out[...] = (rotated.astype(jnp.bfloat16).astype(jnp.float32) * SCORE_SCALE).astype(
        jnp.bfloat16
    )
    key_out[...] = rotate_lanes(key[...], cosine[...], sine[...], 1.0).astype(jnp.bfloat16)
    value_out[...] = value[...].astype(jnp.bfloat16)
    turned_values = value[...].T.astype(jnp.bfloat16)
    heads = query.shape[1] // HEAD_WIDTH
    share = heads * HEAD_WIDTH // key.shape[1]
    outputs = []
    for head in range(heads):
        lanes = slice(head * HEAD_WIDTH, (head + 1) * HEAD_WIDTH)
        group = slice(head // share * HEAD_WIDTH, (head // share + 1) * HEAD_WIDTH)
        scores = cross_dot(key_out[:, group], query_out[:, lanes]) + bias[...]
        top = jnp.max(scores, axis=0, keepdims=True)
        weights = jnp.exp(scores - top)
        total = jnp.sum(weights, axis=0, keepdims=True)
        logsum_out[head : head + 1, :] = top + jnp.log(total)
        attend = (weights * (1.0 / total)).astype(jnp.bfloat16)
        outputs.append(
            jnp.dot(turned_values[group], attend, preferred_element_type=jnp.float32)
        )
    mixed_out[...] = jnp.concatenate(outputs, axis=0).T.astype(jnp.bfloat16)


def attend_backward(
    query, key, value, mixed_grad, logsum, cosine, sine, key_ids, query_ids, query_out, key_out,
    value_out, bias,
):
    set_bias(bias, key_ids, query_ids)
    heads = query.shape[1] // HEAD_WIDTH
    groups = key.shape[1] // HEAD_WIDTH
    share = heads // groups
    turned_keys = key[...].astype(jnp.float32).T.astype(jnp.bfloat16)
    query_grads = []
    key_grads = []
    value_grads = []
    for group_index in range(groups):
        group = slice(group_index * HEAD_WIDTH, (group_index + 1) * HEAD_WIDTH)
        key_grad = value_grad = None
        for head in range(group_index * share, (group_index + 1) * share):
            lanes = slice(head * HEAD_WIDTH, (head + 1) * HEAD_WIDTH)
            scores = cross_dot(key[:, group], query[:, lanes]) + bias[...]
            attend = jnp.exp(scores - logsum[head : head + 1, :])
            attend_grad = cross_dot(value[:, group], mixed_grad[:, lanes])
            delta = jnp.sum(attend * attend_grad, axis=0, keepdims=True)
            score_grad = (attend * (attend_grad - delta)).astype(jnp.bfloat16)
            value_term = matrix_product(attend.astype(jnp.bfloat16), mixed_grad[:, lanes])
            key_term = matrix_product(score_grad, query[:, lanes])
            value_grad = value_term if value_grad is None else value_grad + value_term
            key_grad = key_term if key_grad is None else key_grad + key_term
            query_grads.append(matrix_product(turned_keys[group], score_grad))
        key_grads.append(key_grad)
        value_grads.append(value_grad)
    query_grad = SCORE_SCALE * jnp.concatenate(query_grads, axis=0).T
    key_grad = jnp.concatenate(key_grads, axis=1)
    query_out[...] = rotate_lanes(query_grad, cosine[...], sine[...], -1.0).astype(jnp.bfloat16)
    key_out[...] = rotate_lanes(key_grad, cosine[...], sine[...], -1.0).astype(jnp.bfloat16)
    value_out[...] = jnp.concatenate(value_grads, axis=1).astype(jnp.bfloat16)


def hidden_backward(wide, grads, down, wide_out):
    hidden = down.shape[0]
    hidden_grad = cross_dot(grads[...], down[...])
    gating, upward = wide[:, :hidden], wide[:, hidden:]
    gate = 1.0 / (1.0 + jnp.exp(-gating))
    active = gating * gate
    wide_out[:, :hidden] = (hidden_grad * upward * (gate + active * (1.0 - gate))).astype(
        jnp.bfloat16
    )
    wide_out[:, hidden:] = (hidden_grad * active).astype(jnp.bfloat16)


def hidden_backward_call(wide, grads, down):
    rows, both = wide.shape
    width = grads.shape[1]
    block = 512

    def rows_of(columns):
        return pl.BlockSpec((block, columns), lambda step: (step, 0))

    return pl.pallas_call(
        hidden_backward,
        grid=(rows // block,),
        in_specs=[
            rows_of(both),
            rows_of(width),
            pl.BlockSpec(down.shape, lambda step: (0, 0)),
        ],
        out_specs=rows_of(both),
        out_shape=jax.ShapeDtypeStruct((rows, both), jnp.bfloat16),
        compiler_params=pltpu.CompilerParams(
            dimension_semantics=("arbitrary",), vmem_limit_bytes=56 * 1024 * 1024
        ),
        cost_estimate=pl.CostEstimate(
            flops=rows * both * width,
            bytes_accessed=rows * (both * 6 + width * 2) + down.size * 2,
            transcendentals=rows * both // 2,
        ),
        name="hb",
    )(wide, grads, down)


def kernel_cost(length, passes):
    return pl.CostEstimate(
        flops=2 * passes * QUERY_HEADS * HEAD_WIDTH * length * length,
        bytes_accessed=12 * length * QUERY_HEADS * HEAD_WIDTH,
        transcendentals=QUERY_HEADS * length * length,
    )


def attention_calls(length):
    step_keys = LANES
    steps = KEY_VALUE_HEADS * HEAD_WIDTH // step_keys
    step_queries = QUERY_HEADS * HEAD_WIDTH // steps
    step_heads = step_queries // HEAD_WIDTH
    key_start = QUERY_HEADS * HEAD_WIDTH // step_keys

    def columns(block, first):
        return pl.BlockSpec((length, block), lambda step: (0, step + first))

    def fixed(*shape):
        return pl.BlockSpec(shape, lambda step: (0, 0))

    tables = [
        fixed(length, LANES),
        fixed(length, LANES),
        fixed(length, 1),
        fixed(1, length),
    ]
    logsum = pl.BlockSpec((step_heads, length), lambda step: (step, 0))
    query_shape = jax.ShapeDtypeStruct((length, QUERY_HEADS * HEAD_WIDTH), jnp.bfloat16)
    key_shape = jax.ShapeDtypeStruct((length, KEY_VALUE_HEADS * HEAD_WIDTH), jnp.bfloat16)
    params = pltpu.CompilerParams(
        dimension_semantics=("arbitrary",), vmem_limit_bytes=48 * 1024 * 1024
    )
    forward = pl.pallas_call(
        attend_forward,
        grid=(steps,),
        in_specs=[
            columns(step_queries, 0),
            columns(step_keys, key_start),
            columns(step_keys, key_start + steps),
            *tables,
        ],
        out_specs=[
            columns(step_queries, 0),
            columns(step_keys, 0),
            columns(step_keys, 0),
            columns(step_queries, 0),
            logsum,
        ],
        out_shape=[
            query_shape,
            key_shape,
            key_shape,
            query_shape,
            jax.ShapeDtypeStruct((QUERY_HEADS, length), jnp.float32),
        ],
        scratch_shapes=[pltpu.VMEM((length, length), jnp.float32)],
        compiler_params=params,
        cost_estimate=kernel_cost(length, 2),
        name="af",
    )
    backward = pl.pallas_call(
        attend_backward,
        grid=(steps,),
        in_specs=[
            columns(step_queries, 0),
            columns(step_keys, 0),
            columns(step_keys, 0),
            columns(step_queries, 0),
            logsum,
            *tables,
        ],
        out_specs=[columns(step_queries, 0), columns(step_keys, 0), columns(step_keys, 0)],
        out_shape=[query_shape, key_shape, key_shape],
        scratch_shapes=[pltpu.VMEM((length, length), jnp.float32)],
        compiler_params=params,
        cost_estimate=kernel_cost(length, 5),
        name="ab",
    )
    return forward, backward


def layer(
    tokens,
    block_ids,
    query_weight,
    key_projection_weight,
    value_projection_weight,
    output_weight,
    gate_weight,
    up_weight,
    down_weight,
    attn_gain,
    mlp_gain,
    cotangent,
):
    token_length, _ = tokens.shape
    row_count, hidden_width = gate_weight.shape
    slow = lax.axis_size(SLOW_AXIS)
    unit = hidden_width // (slow * 8)
    local_hidden = slow * unit
    query_width = query_weight.shape[1]
    key_width = key_projection_weight.shape[1]
    qkv_width = query_width + 2 * key_width
    first_replica = lax.axis_index(REPLICA_AXIS) == 0
    first_chip = lax.axis_index(CHIP_AXIS) == 0
    first_core = lax.axis_index(CORE_AXIS) == 0

    gain_columns = jnp.pad(
        jnp.stack([attn_gain, mlp_gain], axis=1), ((0, 0), (0, LANES - 2))
    )
    qkv_local = jnp.concatenate(
        [query_weight, key_projection_weight, value_projection_weight, gain_columns], axis=1
    )
    qkv_all = gather_weight(qkv_local)
    output_all = gather_weight(output_weight)

    def column_slices(weight, member):
        pieces = []
        for step in range(slow):
            start = (step * 4 + member) * 2 * unit
            pieces.append(
                jnp.where(
                    first_replica,
                    weight[:, start : start + unit],
                    weight[:, start + unit : start + 2 * unit],
                )
            )
        return pieces

    packed = [
        jnp.concatenate(
            column_slices(gate_weight, member) + column_slices(up_weight, member), axis=1
        )
        for member in range(4)
    ]
    near, far = order(
        first_chip,
        jnp.concatenate(packed[:2], axis=0),
        jnp.concatenate(packed[2:], axis=0),
    )
    wide_blocks = []
    for block in order(first_chip, near, swap(far, CHIP_AXIS)):
        near, far = order(first_core, block[:row_count], block[row_count:])
        wide_blocks.extend(order(first_core, near, swap(far, CORE_AXIS)))
    wide_local = jnp.concatenate(wide_blocks, axis=0)
    down_local = jnp.where(first_replica, down_weight[:unit], down_weight[unit:])
    wide_all = lax.all_gather(wide_local, SLOW_AXIS, axis=0, tiled=True)
    down_all = lax.all_gather(down_local, SLOW_AXIS, axis=0, tiled=True)

    gains = qkv_all[:, qkv_width:][:, :2].T.astype(jnp.float32)
    attn_scale, mlp_scale = gains[0], gains[1]
    inputs = tokens.astype(jnp.float32)
    cosine_table, sine_table = rope_tables(token_length, HEAD_WIDTH)
    signs = jnp.where(jnp.arange(HEAD_WIDTH) < HEAD_WIDTH // 2, -1.0, 1.0)
    tables = (
        jnp.tile(cosine_table, (1, LANES // HEAD_WIDTH)),
        jnp.tile(sine_table * signs, (1, LANES // HEAD_WIDTH)),
        block_ids.T,
        block_ids,
    )
    attend_forward_call, attend_backward_call = attention_calls(token_length)
    first_normed = rms_norm(inputs, attn_scale).astype(jnp.bfloat16)
    projected = matrix_product(first_normed, qkv_all)
    query_rows, key_rows, value_rows, mixed, logsum = attend_forward_call(
        projected, projected, projected, *tables
    )
    attn_out = matrix_product(mixed, output_all)
    residual = inputs + RESIDUAL * attn_out
    normed2 = rms_norm(residual, mlp_scale).astype(jnp.bfloat16)
    plane, partners = gather_tokens(normed2)
    normed2_all = jnp.concatenate(plane + partners, axis=0)
    grad_out = cotangent.astype(jnp.float32)
    down_in = (RESIDUAL * grad_out).astype(jnp.bfloat16)
    plane, partners = gather_tokens(down_in)
    down_in_all = jnp.concatenate(plane + partners, axis=0)
    wide = matrix_product(normed2_all, wide_all)
    gating, upward = wide[:, :local_hidden], wide[:, local_hidden:]
    hidden_act = (jax.nn.silu(gating) * upward).astype(jnp.bfloat16)
    grad_down = narrow(contract_rows(hidden_act, down_in_all))
    down_part = lax.psum_scatter(grad_down, SLOW_AXIS, scatter_dimension=0, tiled=True)

    def pieces_of(plane_rows):
        return [plane_rows[i * token_length : (i + 1) * token_length] for i in range(4)]

    def to_owners(rows, weight, product):
        partner = narrow(product(rows[4 * token_length :], weight))
        mine = narrow(product(rows[: 4 * token_length], weight))
        return scatter_pieces(pieces_of(mine), pieces_of(partner))

    mlp_out = to_owners(hidden_act, down_all, matrix_product)
    output = (residual + RESIDUAL * mlp_out).astype(jnp.bfloat16)
    wide_in = hidden_backward_call(wide, down_in_all, down_all)
    normed2_grad = to_owners(wide_in, wide_all, contract_cols)
    parts = []
    for start in (0, local_hidden):
        grad = narrow(contract_rows(normed2_all, wide_in[:, start : start + local_hidden]))
        parts.append(lax.psum_scatter(grad, SLOW_AXIS, scatter_dimension=0, tiled=True))

    def exchange(part):
        near, far = order(first_chip, part[: 2 * row_count], part[2 * row_count :])
        low, high = order(first_chip, near, swap(far, CHIP_AXIS))
        members = []
        for block in (low, high):
            near, far = order(first_core, block[:row_count], block[row_count:])
            members.extend(order(first_core, near, swap(far, CORE_AXIS)))
        members = jnp.concatenate(members, axis=0)
        sources = order(first_replica, members, swap(members, REPLICA_AXIS))
        pieces = []
        for step in range(slow):
            for member in range(4):
                for source in sources:
                    pieces.append(
                        source[
                            member * row_count : (member + 1) * row_count,
                            step * unit : (step + 1) * unit,
                        ]
                    )
        return jnp.concatenate(pieces, axis=1).astype(jnp.float32)

    gate_shard, up_shard = exchange(parts[0]), exchange(parts[1])
    down_shard = jnp.concatenate(
        order(first_replica, down_part, swap(down_part, REPLICA_AXIS)), axis=0
    ).astype(jnp.float32)

    _, norm2_pull = jax.vjp(rms_norm, residual, mlp_scale)
    residual_part, grad_mlp_gain = norm2_pull(normed2_grad)
    residual_grad = grad_out + residual_part

    def member_columns(left):
        blocks = {}
        for chip in range(2):
            for core in range(2):
                blocks[chip, core] = jnp.concatenate(
                    [
                        left[:, start : start + row_count]
                        for start in (
                            (step * 4 + chip * 2 + core) * row_count for step in range(slow)
                        )
                    ],
                    axis=1,
                )
        near = [order(first_chip, blocks[0, core], blocks[1, core]) for core in range(2)]
        chips = [order(first_core, near[0][chip], near[1][chip]) for chip in range(2)]
        return [[chips[chip][core] for chip in range(2)] for core in range(2)]

    def weight_part(left, right):
        half = right.shape[1] // 2
        sides = order(first_replica, right[:, :half], right[:, half:])
        blocks = member_columns(left)
        products = []
        for chips in (blocks[1], blocks[0]):
            products.append(
                [
                    narrow(contract_rows(chips[chip], sides[side]))
                    for side, chip in ((0, 0), (0, 1), (1, 0), (1, 1))
                ]
            )
        partner, mine = products
        return narrow(scatter_pieces(mine, partner))

    def both_sides(part):
        return jnp.concatenate(
            order(first_replica, part, swap(part, REPLICA_AXIS)), axis=1
        ).astype(jnp.float32)

    attn_in = (RESIDUAL * residual_grad).astype(jnp.bfloat16)
    output_part = weight_part(mixed, attn_in)
    output_part = lax.psum_scatter(output_part, SLOW_AXIS, scatter_dimension=0, tiled=True)
    output_shard = both_sides(output_part)
    mixed_grad = contract_cols(attn_in, output_all).astype(jnp.bfloat16)
    query_lin_grad, key_lin_grad, value_lin_grad = attend_backward_call(
        query_rows, key_rows, value_rows, mixed_grad, logsum, *tables
    )
    qkv_in = jnp.concatenate([query_lin_grad, key_lin_grad, value_lin_grad], axis=1)
    qkv_sum = weight_part(first_normed, qkv_in)
    normed1_grad = contract_cols(qkv_in, qkv_all[:, :qkv_width])
    _, norm1_pull = jax.vjp(rms_norm, inputs, attn_scale)
    input_part, grad_attn_gain = norm1_pull(normed1_grad)
    input_grad = residual_grad + input_part
    gain_grads = jnp.stack([grad_attn_gain, grad_mlp_gain], axis=0)
    for axis in (CORE_AXIS, CHIP_AXIS, REPLICA_AXIS):
        gain_grads = gain_grads + swap(gain_grads, axis)
    gain_rows = jnp.pad(member_columns(gain_grads)[0][0].T, ((0, 0), (0, LANES - 2)))
    qkv_sum = jnp.concatenate([qkv_sum, gain_rows.astype(jnp.bfloat16)], axis=1)
    qkv_part = lax.psum_scatter(qkv_sum, SLOW_AXIS, scatter_dimension=0, tiled=True)
    qkv_shard = both_sides(qkv_part[:, : qkv_width // 2])
    attn_gain_shard = qkv_part[:, qkv_width // 2].astype(jnp.float32)
    mlp_gain_shard = qkv_part[:, qkv_width // 2 + 1].astype(jnp.float32)
    return (
        output,
        input_grad,
        qkv_shard[:, :query_width],
        qkv_shard[:, query_width : query_width + key_width],
        qkv_shard[:, query_width + key_width :],
        output_shard,
        gate_shard,
        up_shard,
        down_shard,
        attn_gain_shard,
        mlp_gain_shard,
    )


def solution(mesh):
    replicas, shard_count = mesh.shape[REPLICA_AXIS], mesh.shape["shard"]
    inner = KEY_VALUE_HEADS // replicas
    cores = 2
    split_mesh = Mesh(
        mesh.devices.reshape(replicas, shard_count // inner, inner // cores, cores),
        (REPLICA_AXIS, *GROUP),
    )
    everyone = P((REPLICA_AXIS, *GROUP), None)
    sharded = P(GROUP, None)
    vector = P(GROUP)
    return jax.shard_map(
        layer,
        mesh=split_mesh,
        in_specs=(everyone, everyone) + (sharded,) * 7 + (vector, vector, everyone),
        out_specs=(everyone, everyone) + (sharded,) * 7 + (vector, vector),
        check_vma=False,
    )
```
